128 devices in a mesh: sub: 8 (over z, core), row: 16 (over x, y).
Axes of the slice: x: 4, y: 4, z: 4, core: 2. Of those that a mesh axis runs over, the one named last changes fastest.
Arguments:
- spectra: bfloat16 [8, 131072, 256], P('sub', 'row')
- mass_blocks: bfloat16 [8, 1024, 9, 128, 128], P('sub', 'row'), may hold values from -0.1875 to 0.1875
- offsets: int32 [8, 1024, 9], P('sub', 'row'), may hold values from -16 to 16
- counts: int32 [8], P('sub'), may hold values from 1 to 131072, 734003 in all
Outputs:
- weighted_modes: bfloat16 [8, 131072, 192], P('sub', 'row')
The draws below stay inside these ranges and needn't reach their ends.
Inputs may be any that keep to these rules, and one draw needn't show every extreme that they name: `counts`: rows at or past a subdomain's count hold no data; the largest count is exactly 131072.
All inputs are finite; a program needn't handle non-finite values. No bound on the sum of `counts` on one device may be relied on, other than what follows from the above.
Results may differ from the reference program's by a relative error of at most 0.001.
The reference program's roundings to bfloat16 on the way (of `masked`, `weighted` and `projector`) count: a program that leaves them out, or rounds other values in their place, can miss the bound.
Values may be sent and summed in bfloat16 or wider, within the bound.
No kernel may reach another device: no remote copies, remote signals or barrier semaphores. Data moves between devices by JAX's collectives and lax.ppermute only.
A program may use at most 256 MiB of HBM per device.

```python
import math
import jax
import jax.numpy as jnp
import numpy as np
from jax import lax

BLK = 64
RANK = 48
FREQ = 2
BS = 128
NBR = 9
ITERS = 5
HB = 16
ROWS = 131072
BLOCKS = 1024
SUBS = 8
COLS = 256


def draw_spectra(key, part):
    key_base, key_rows, key_cols = jax.random.split(key, 3)
    row_scale = jnp.exp(jax.random.uniform(key_rows, (SUBS, ROWS, 1), jnp.float32, math.log(0.3), math.log(3.0)))
    col_scale = jnp.exp(jax.random.uniform(key_cols, (1, 1, COLS), jnp.float32, math.log(0.4), math.log(4.0)))
    base = jax.random.normal(key_base, (SUBS, ROWS, COLS), jnp.float32)
    values = jnp.clip(base * row_scale * col_scale, -40.0, 40.0)
    return values.astype(jnp.bfloat16)


def touch_ends(drawn, own_key, least, largest):
    spot = [jax.random.randint(jax.random.fold_in(own_key, axis), (), 0, length) for axis, length in enumerate(drawn.shape)]
    main_axis = drawn.shape.index(max(drawn.shape))
    neighbour = spot[:main_axis] + [(spot[main_axis] + 1) % drawn.shape[main_axis]] + spot[main_axis + 1:]
    return drawn.at[tuple(spot)].set(least).at[tuple(neighbour)].set(largest)


def shard_levels(stream_key, dims, pieces, least, top_value):
    def one(axis_at, blocks):
        draws = jax.random.uniform(jax.random.fold_in(jax.random.fold_in(stream_key, 6), axis_at), (blocks,), jnp.float32, least / len(pieces), top_value / len(pieces))
        return jnp.repeat(jnp.exp(draws), dims[axis_at] // blocks).reshape((-1,) + (1,) * (len(dims) - axis_at - 1))

    level = one(*pieces[0])
    for cut in pieces[1:]:
        level = level * one(*cut)
    return level


def profile(amount, total, limit, lean):
    portions = [(1 << 20) // math.isqrt(grade ** lean) + 1 for grade in range(2, amount + 1)]
    surplus, given = total - limit - (amount - 1), [1] * (amount - 1)
    while surplus > 0:
        movable = [i for i in range(amount - 1) if given[i] < limit]
        pool, left = sum([portions[i] for i in movable]), surplus
        for i in movable:
            extra = min(limit - given[i], max(1, left * portions[i] // pool), surplus)
            given[i] = given[i] + extra
            surplus = surplus - extra
    return np.array([limit] + given)


def ragged_sizes(rng, count, total, bound, skew):
    if count == 2:
        one = jax.random.randint(rng, (), max(1, total - bound), min(bound, total - 1) + 1)
        return jnp.stack([one, total - one])
    sizes = jnp.asarray(profile(count, total, bound, skew), jnp.int32)
    couples = (count - 1) // 2
    giver, receiver = sizes[1:1 + 2 * couples:2], sizes[2:2 + 2 * couples:2]
    margin = jnp.minimum(giver - 1, bound - receiver)
    shifted = jax.random.randint(jax.random.fold_in(rng, 1), (couples,), 0, 1 << 20) % (margin + 1)
    sizes = sizes.at[1:1 + 2 * couples:2].set(giver - shifted).at[2:2 + 2 * couples:2].set(receiver + shifted)
    return sizes[jax.random.permutation(jax.random.fold_in(rng, 2), count)]


def centred(key, extent, spread, reach, pieces=(), kind=jnp.bfloat16):
    gain = shard_levels(key, extent, pieces, -0.22, 0.18) if pieces else 1.0
    drawn = jax.random.normal(key, extent, jnp.float32) * spread * gain
    return jnp.minimum(jnp.maximum(drawn, -reach), reach).astype(kind)


def setup_inputs(seed: int = 0) -> dict:
    streams_of = jax.random.split(jax.random.key(seed), 5)
    spectra = draw_spectra(jax.random.fold_in(streams_of[4], 71), 0)
    mass_blocks = centred(streams_of[1], (SUBS, BLOCKS, NBR, BS, BS), (NBR * BS) ** -0.5, 0.1875, ((0, 8), (1, 16)))
    offsets = touch_ends(jax.random.randint(streams_of[2], (SUBS, BLOCKS, NBR), 0 - HB, HB + 1), jax.random.fold_in(streams_of[2], 1), 0 - HB, HB).astype(jnp.int32)
    counts = ragged_sizes(streams_of[3], SUBS, SUBS * ROWS * 7 // 10, ROWS, 0).astype(jnp.int32)
    return {"spectra": spectra, "mass_blocks": mass_blocks, "offsets": offsets, "counts": counts}


def weigh_subdomain(spectra_sub, mass_sub, offsets_sub, live_count):
    row_count = spectra_sub.shape[0]
    live_rows = (jnp.arange(row_count, dtype=jnp.int32) < live_count)[:, None]
    masked = jnp.where(live_rows, spectra_sub, jnp.zeros((), spectra_sub.dtype))
    halo_rows = HB * BS
    padded = jnp.pad(masked, ((halo_rows, halo_rows), (0, 0)))
    block_count = row_count // BS
    blocks = padded.reshape(block_count + 2 * HB, BS, COLS)
    block_index = (jnp.arange(block_count, dtype=jnp.int32)[:, None] + offsets_sub + HB).astype(jnp.int32)
    summed = jnp.zeros((block_count, BS, COLS), jnp.float32)
    for slot in range(NBR):
        picked = jnp.take(blocks, block_index[:, slot], axis=0).astype(jnp.float32)
        summed = summed + jnp.einsum('bij,bjc->bic', mass_sub[:, slot].astype(jnp.float32), picked)
    weighted = jnp.where(live_rows, summed.reshape(row_count, COLS), 0.0).astype(jnp.bfloat16)
    columns = weighted.reshape(row_count, FREQ, 2 * BLK).astype(jnp.float32)
    gram = jnp.einsum('rfc,rfd->fcd', columns, columns)
    return (weighted, gram)

def whiten(gram):
    half_width = BLK
    g_real = gram[:, :half_width, :half_width] + gram[:, half_width:, half_width:]
    g_imag = gram[:, :half_width, half_width:] - gram[:, half_width:, :half_width]
    realified = jnp.concatenate([jnp.concatenate([g_real, -g_imag], 2), jnp.concatenate([g_imag, g_real], 2)], 1)
    scaled = realified / jnp.sqrt(lax.optimization_barrier(jnp.sum(realified * realified, axis=(1, 2), keepdims=True)) + 1e-06)
    identity = jnp.broadcast_to(jnp.eye(2 * half_width, dtype=jnp.float32), scaled.shape)
    iterate = scaled
    whitener = identity
    for step in range(ITERS):
        correction = 1.5 * identity - 0.5 * jnp.einsum('fij,fjk->fik', whitener, iterate, precision=lax.Precision.HIGHEST)
        iterate = jnp.einsum('fij,fjk->fik', iterate, correction, precision=lax.Precision.HIGHEST)
        whitener = jnp.einsum('fij,fjk->fik', correction, whitener, precision=lax.Precision.HIGHEST)
    r_real = whitener[:, :half_width, :RANK]
    r_imag = whitener[:, half_width:, :RANK]
    projector = jnp.concatenate([jnp.concatenate([r_real, r_imag], 2), jnp.concatenate([-r_imag, r_real], 2)], 1)
    return projector.astype(jnp.bfloat16)

def reference(spectra, mass_blocks, offsets, counts):

    def one_subdomain(items):
        return weigh_subdomain(items[0], items[1], items[2], items[3])
    weighted, grams = lax.map(one_subdomain, (spectra, mass_blocks, offsets, counts))
    gram = lax.optimization_barrier(jnp.sum(grams, axis=0))
    projector = whiten(gram).astype(jnp.float32)

    def project(weighted_sub):
        columns = weighted_sub.reshape(ROWS, FREQ, 2 * BLK).astype(jnp.float32)
        modes = jnp.einsum('rfc,fcd->rfd', columns, projector)
        return modes.reshape(ROWS, FREQ * 2 * RANK).astype(jnp.bfloat16)
    return lax.map(project, weighted)
```

```python
import functools

import jax
import jax.numpy as jnp
from jax import lax
from jax.experimental import pallas as pl
from jax.experimental.pallas import tpu as pltpu
from jax.sharding import Mesh
from jax.sharding import PartitionSpec as P

BLK = 64
RANK = 48
FREQ = 2
ITERS = 5
HB = 16
BS = 128
GROUP = 4
CHUNK = 1024
SUB = ("z", "c")
ROW = ("x", "y")


def fill_blocks(rel, copies, xs, lo, hi):
    for copy in copies:
        copy.start()
    spare = xs.shape[0] - 1
    xs[spare] = jnp.zeros(xs.shape[1:], xs.dtype)
    for copy in copies:
        copy.wait()
    end = rel + HB * BS
    cut = lax.shift_right_arithmetic(end, 7)
    kept = jnp.bitwise_and(end, BS - 1)

    @pl.when((kept > 0) & (cut >= lo) & (cut < hi))
    def _():
        rows = lax.broadcasted_iota(jnp.int32, xs.shape[1:], 0)
        block = xs[cut]
        xs[cut] = jnp.where(rows < kept, block, jnp.zeros_like(block))


def weigh_group(idx_ref, rel, first, mass_ref, xs, zt_ref, gram):
    slots = mass_ref.shape[1]
    rows = lax.broadcasted_iota(jnp.int32, (BS, xs.shape[2]), 0)
    parts = []
    for r in range(mass_ref.shape[0]):
        b = first + r
        left = jnp.concatenate([mass_ref[r, k] for k in range(slots)], axis=1)
        right = jnp.concatenate([xs[idx_ref[k, b]] for k in range(slots)], axis=0)
        acc = jnp.dot(left, right, preferred_element_type=jnp.float32)
        parts.append(jnp.where(rows < rel - b * BS, acc, 0.0).astype(jnp.bfloat16))
    z = jnp.concatenate(parts, axis=0)
    zt = z.T
    zt_ref[...] = zt
    for f in range(FREQ):
        s = slice(f * 2 * BLK, (f + 1) * 2 * BLK)
        gram[f] += jnp.dot(zt[s], z[:, s], preferred_element_type=jnp.float32)


def inner_kernel(idx_ref, rel_ref, mass_ref, sp_ref, zt_ref, gram_ref, xs, sem):
    step = pl.program_id(0)
    rel = rel_ref[0]
    local = sp_ref.shape[0]

    @pl.when(step == 0)
    def _():
        gram_ref[...] = jnp.zeros_like(gram_ref)
        copies = [pltpu.make_async_copy(sp_ref, xs.at[pl.ds(HB, local)], sem.at[0])]
        fill_blocks(rel, copies, xs, HB, HB + local)

    weigh_group(idx_ref, rel, HB + step * GROUP, mass_ref, xs, zt_ref, gram_ref)


def edge_kernel(idx_ref, rel_ref, mass_ref, sp_ref, prev_ref, next_ref, part_ref, zt_in, zt_ref, packed_ref, xs, gram, sem):
    del zt_in
    step = pl.program_id(0)
    rel = rel_ref[0]
    local = sp_ref.shape[0]
    half = HB // GROUP

    @pl.when(step == 0)
    def _():
        gram[...] = part_ref[...]
        copies = [
            pltpu.make_async_copy(prev_ref, xs.at[pl.ds(0, HB)], sem.at[0]),
            pltpu.make_async_copy(sp_ref, xs.at[pl.ds(HB, local)], sem.at[1]),
            pltpu.make_async_copy(next_ref, xs.at[pl.ds(HB + local, HB)], sem.at[2]),
        ]
        fill_blocks(rel, copies, xs, 0, 2 * HB + local)

    first = jnp.where(step < half, step * GROUP, local - 2 * HB + step * GROUP)
    weigh_group(idx_ref, rel, first, mass_ref, xs, zt_ref, gram)

    @pl.when(step == pl.num_programs(0) - 1)
    def _():
        i = lax.broadcasted_iota(jnp.int32, (BLK, BLK), 0)
        j = lax.broadcasted_iota(jnp.int32, (BLK, BLK), 1)
        packs = []
        for f in range(FREQ):
            h = gram[f]
            g_real = h[:BLK, :BLK] + h[BLK:, BLK:]
            g_imag = h[:BLK, BLK:] - h[BLK:, :BLK]
            packs.append(jnp.where(i <= j, g_real, g_imag))
        packed_ref[...] = jnp.concatenate(packs, axis=1)


def whiten_packed(packed):
    i = lax.broadcasted_iota(jnp.int32, (BLK, BLK), 0)
    j = lax.broadcasted_iota(jnp.int32, (BLK, BLK), 1)
    turned = packed.T
    g_real = jnp.where(i <= j, packed, turned)
    g_imag = jnp.where(i > j, packed, jnp.where(i < j, -turned, 0.0))
    realified = jnp.concatenate(
        [jnp.concatenate([g_real, -g_imag], 1), jnp.concatenate([g_imag, g_real], 1)], 0
    )
    total = jnp.sum(jnp.sum(realified * realified, axis=1, keepdims=True), axis=0, keepdims=True)
    return realified / jnp.sqrt(total + 1e-06)


def product(a, b):
    return jnp.dot(a, b, precision=lax.Precision.HIGHEST, preferred_element_type=jnp.float32)


def project_kernel(packed_ref, zt_ref, out_ref, zt, out, in_sem, out_sem):
    n = zt.shape[1] // CHUNK

    def fetch(c):
        s = pl.ds(c * CHUNK, CHUNK)
        return pltpu.make_async_copy(zt_ref.at[:, s], zt.at[:, s], in_sem.at[c])

    def send(c):
        s = pl.ds(c * CHUNK, CHUNK)
        return pltpu.make_async_copy(out.at[:, s], out_ref.at[:, s], out_sem.at[c])

    for c in range(n):
        fetch(c).start()
    size = 2 * BLK
    i = lax.broadcasted_iota(jnp.int32, (size, size), 0)
    j = lax.broadcasted_iota(jnp.int32, (size, size), 1)
    eye = jnp.where(i == j, 1.5, 0.0)
    packed = packed_ref[...]
    ys = [whiten_packed(packed[:, f * BLK : (f + 1) * BLK]) for f in range(FREQ)]
    cs = [eye - 0.5 * y for y in ys]
    ys = [product(y, c) for y, c in zip(ys, cs)]
    xs = cs
    for step in range(1, ITERS):
        cs = [eye - 0.5 * product(x, y) for x, y in zip(xs, ys)]
        if step < ITERS - 1:
            ys = [product(y, c) for y, c in zip(ys, cs)]
        xs = [product(c, x) for c, x in zip(cs, xs)]
    projectors = []
    for x in xs:
        top = x.T[:RANK]
        re, im = top[:, :BLK], top[:, BLK:]
        projectors.append(
            jnp.concatenate(
                [jnp.concatenate([re, -im], 1), jnp.concatenate([im, re], 1)], 0
            ).astype(jnp.bfloat16)
        )
    wide = 2 * RANK
    for c in range(n):
        fetch(c).wait()
        s = slice(c * CHUNK, (c + 1) * CHUNK)
        for f in range(FREQ):
            out[f * wide : (f + 1) * wide, s] = jnp.dot(
                projectors[f], zt[f * size : (f + 1) * size, s], preferred_element_type=jnp.float32
            ).astype(jnp.bfloat16)
        send(c).start()
    for c in range(n):
        send(c).wait()


def all_sum(value, axis):
    n = lax.axis_size(axis)
    others = [lax.ppermute(value, axis, [(i, (i + k) % n) for i in range(n)]) for k in range(1, n)]
    for other in others:
        value = value + other
    return value


def local(spectra, mass_blocks, offsets, counts):
    rows, cols = spectra.shape[1:]
    blocks = rows // BS
    slots = mass_blocks.shape[2]
    devices = lax.axis_size(ROW)
    sp = spectra[0].reshape(blocks, BS, cols)
    up = [(i, i + 1) for i in range(devices - 1)]
    down = [(j, i) for i, j in up]
    before = lax.ppermute(sp[blocks - HB :], ROW, up)
    after = lax.ppermute(sp[:HB], ROW, down)

    rel = counts - lax.axis_index(ROW) * rows
    place = jnp.arange(blocks, dtype=jnp.int32)[None, :] + offsets[0].T
    index = jnp.where(place * BS < rel[0], place + HB, blocks + 2 * HB).astype(jnp.int32)
    mass = mass_blocks[0]
    width = GROUP * BS
    inner = blocks - 2 * HB
    xs_shape = pltpu.VMEM((blocks + 2 * HB + 1, BS, cols), jnp.bfloat16)
    mass_block = (GROUP, slots, BS, BS)
    anywhere = pl.BlockSpec(memory_space=pl.ANY)
    gram_shape = (FREQ, 2 * BLK, 2 * BLK)

    zt, part = pl.pallas_call(
        inner_kernel,
        out_shape=(
            jax.ShapeDtypeStruct((cols, rows), jnp.bfloat16),
            jax.ShapeDtypeStruct(gram_shape, jnp.float32),
        ),
        grid_spec=pltpu.PrefetchScalarGridSpec(
            num_scalar_prefetch=2,
            grid=(inner // GROUP,),
            in_specs=[
                pl.BlockSpec(mass_block, lambda s, *_: (s + HB // GROUP, 0, 0, 0)),
                anywhere,
            ],
            out_specs=[
                pl.BlockSpec((cols, width), lambda s, *_: (0, s + HB // GROUP)),
                pl.BlockSpec(gram_shape, lambda s, *_: (0, 0, 0)),
            ],
            scratch_shapes=[xs_shape, pltpu.SemaphoreType.DMA((1,))],
        ),
        name="inner_rows",
    )(index, rel, mass, sp)

    half = HB // GROUP
    edge_block = lambda s: jnp.where(s < half, s, blocks // GROUP - 2 * half + s)
    zt, packed = pl.pallas_call(
        edge_kernel,
        out_shape=(
            jax.ShapeDtypeStruct((cols, rows), jnp.bfloat16),
            jax.ShapeDtypeStruct((BLK, 2 * BLK), jnp.float32),
        ),
        grid_spec=pltpu.PrefetchScalarGridSpec(
            num_scalar_prefetch=2,
            grid=(2 * half,),
            in_specs=[
                pl.BlockSpec(mass_block, lambda s, *_: (edge_block(s), 0, 0, 0)),
                anywhere,
                anywhere,
                anywhere,
                pl.BlockSpec(gram_shape, lambda s, *_: (0, 0, 0)),
                anywhere,
            ],
            out_specs=[
                pl.BlockSpec((cols, width), lambda s, *_: (0, edge_block(s))),
                pl.BlockSpec((BLK, 2 * BLK), lambda s, *_: (0, 0)),
            ],
            scratch_shapes=[
                xs_shape,
                pltpu.VMEM(gram_shape, jnp.float32),
                pltpu.SemaphoreType.DMA((3,)),
            ],
        ),
        input_output_aliases={7: 0},
        name="edge_rows",
    )(index, rel, mass, sp, before, after, part, zt)

    for axis in ("c", "y", "x", "z"):
        packed = all_sum(packed, axis)

    count = rows // CHUNK
    out_rows = FREQ * 2 * RANK
    modes = pl.pallas_call(
        project_kernel,
        out_shape=jax.ShapeDtypeStruct((out_rows, rows), jnp.bfloat16),
        in_specs=[pl.BlockSpec(memory_space=pltpu.VMEM), anywhere],
        out_specs=anywhere,
        scratch_shapes=[
            pltpu.VMEM((cols, rows), jnp.bfloat16),
            pltpu.VMEM((out_rows, rows), jnp.bfloat16),
            pltpu.SemaphoreType.DMA((count,)),
            pltpu.SemaphoreType.DMA((count,)),
        ],
        name="whiten_project",
    )(packed, zt)
    return modes.T[None]


def solution(mesh):
    finer = Mesh(mesh.devices.reshape(4, 2, 4, 4), ("z", "c", "x", "y"))
    return jax.shard_map(
        local,
        mesh=finer,
        in_specs=(
            P(SUB, ROW, None),
            P(SUB, ROW, None, None, None),
            P(SUB, ROW, None),
            P(SUB),
        ),
        out_specs=P(SUB, ROW, None),
        check_vma=False,
    )
```

```python
import functools

import jax
import jax.numpy as jnp
from jax import lax
from jax.experimental import pallas as pl
from jax.experimental.pallas import tpu as pltpu
from jax.sharding import Mesh
from jax.sharding import PartitionSpec as P

BLK = 64
RANK = 48
FREQ = 2
ITERS = 5
HB = 16
BS = 128
GROUP = 4
FAR = 4
CHUNK = 1024
SUB = ("z", "c")
ROW = ("x", "y")


def cut_block(rel, xs, spans):
    end = rel + HB * BS
    cut = lax.shift_right_arithmetic(end, 7)
    kept = jnp.bitwise_and(end, BS - 1)
    inside = functools.reduce(jnp.logical_or, [(cut >= lo) & (cut < hi) for lo, hi in spans])

    @pl.when((kept > 0) & inside)
    def _():
        rows = lax.broadcasted_iota(jnp.int32, xs.shape[1:], 0)
        block = xs[cut]
        xs[cut] = jnp.where(rows < kept, block, jnp.zeros_like(block))


def sender(zt, zt_ref, sem, g):
    s = pl.ds(pl.multiple_of(g * GROUP * BS, GROUP * BS), GROUP * BS)
    return pltpu.make_async_copy(zt.at[:, s], zt_ref.at[:, s], sem.at[g])


def weigh_group(idx_ref, rel, first, g, mass, xs, zt_ref, gram):
    slots = mass.shape[1]
    rows = lax.broadcasted_iota(jnp.int32, (BS, xs.shape[2]), 0)
    parts = []
    for r in range(GROUP):
        b = first + r
        left = jnp.concatenate([mass[r, k] for k in range(slots)], axis=1)
        right = jnp.concatenate([xs[idx_ref[k, b]] for k in range(slots)], axis=0)
        acc = jnp.dot(left, right, preferred_element_type=jnp.float32)
        parts.append(jnp.where(rows < rel - b * BS, acc, 0.0).astype(jnp.bfloat16))
    z = jnp.concatenate(parts, axis=0)
    zt = z.T
    zt_ref[:, pl.ds(pl.multiple_of(g * GROUP * BS, GROUP * BS), GROUP * BS)] = zt
    for f in range(FREQ):
        s = slice(f * 2 * BLK, (f + 1) * 2 * BLK)
        gram[f] += jnp.dot(zt[s], z[:, s], preferred_element_type=jnp.float32)


def inner_kernel(idx_ref, rel_ref, mass_ref, sp_ref, zt_ref, gram_ref, xs, edge, mass, zt, x_sem, sem, edge_sem, out_sem):
    rel = rel_ref[0]
    local = sp_ref.shape[0]
    groups = mass.shape[0] // GROUP

    fetch_x = pltpu.make_async_copy(sp_ref, xs.at[pl.ds(HB, local)], x_sem)

    def fetch(g):
        return pltpu.make_async_copy(
            mass_ref.at[pl.ds(HB + g * GROUP, GROUP)], mass.at[pl.ds(g * GROUP, GROUP)], sem.at[g]
        )

    sides = [
        pltpu.make_async_copy(mass_ref.at[pl.ds(0, HB)], edge.at[pl.ds(0, HB)], edge_sem.at[0]),
        pltpu.make_async_copy(
            mass_ref.at[pl.ds(local - HB, HB)], edge.at[pl.ds(HB, HB)], edge_sem.at[1]
        ),
    ]
    fetch_x.start()
    for g in range(groups):
        fetch(g).start()
    for side in sides:
        side.start()
    gram_ref[...] = jnp.zeros_like(gram_ref)
    spare = xs.shape[0] - 1
    xs[spare] = jnp.zeros(xs.shape[1:], xs.dtype)
    fetch_x.wait()
    cut_block(rel, xs, [(HB, HB + local)])

    @pl.loop(0, groups)
    def _(g):
        fetch(g).wait()
        weigh_group(
            idx_ref, rel, HB + g * GROUP, g, mass.at[pl.ds(g * GROUP, GROUP)], xs, zt, gram_ref
        )
        sender(zt, zt_ref, out_sem, g).start()

    for side in sides:
        side.wait()
    for g in range(groups):
        sender(zt, zt_ref, out_sem, g).wait()


def edge_kernel(
    groups, lo, stride, width, idx_ref, rel_ref, edge, prev_ref, next_ref, part_ref, xs_in, xs, zt_ref, gram_ref, gram, zt, sem, out_sem
):
    del xs_in
    rel = rel_ref[0]
    local = xs.shape[0] - 1 - 2 * HB
    low = 0 if width == FAR else FAR
    high = HB + local + (HB - FAR if width == FAR else 0)
    copies = [
        pltpu.make_async_copy(prev_ref, xs.at[pl.ds(low, width)], sem.at[0]),
        pltpu.make_async_copy(next_ref, xs.at[pl.ds(high, width)], sem.at[1]),
    ]
    for copy in copies:
        copy.start()
    gram[...] = part_ref[...]
    for copy in copies:
        copy.wait()
    cut_block(rel, xs, [(low, low + width), (high, high + width)])

    @pl.loop(0, groups)
    def _(g):
        place = lo + g * stride
        first = jnp.where(place < HB // GROUP, place * GROUP, local - 2 * HB + place * GROUP)
        weigh_group(idx_ref, rel, first, g, edge.at[pl.ds(place * GROUP, GROUP)], xs, zt, gram)
        sender(zt, zt_ref, out_sem, g).start()

    if width == FAR:
        gram_ref[...] = pack(gram)
    else:
        gram_ref[...] = gram[...]
    for g in range(groups):
        sender(zt, zt_ref, out_sem, g).wait()


def pack(gram):
    i = lax.broadcasted_iota(jnp.int32, (BLK, BLK), 0)
    j = lax.broadcasted_iota(jnp.int32, (BLK, BLK), 1)
    packs = []
    for f in range(FREQ):
        h = gram[f]
        g_real = h[:BLK, :BLK] + h[BLK:, BLK:]
        g_imag = h[:BLK, BLK:] - h[BLK:, :BLK]
        packs.append(jnp.where(i <= j, g_real, g_imag))
    return jnp.concatenate(packs, axis=1)


def whiten_packed(packed):
    i = lax.broadcasted_iota(jnp.int32, (BLK, BLK), 0)
    j = lax.broadcasted_iota(jnp.int32, (BLK, BLK), 1)
    turned = packed.T
    g_real = jnp.where(i <= j, packed, turned)
    g_imag = jnp.where(i > j, packed, jnp.where(i < j, -turned, 0.0))
    realified = jnp.concatenate(
        [jnp.concatenate([g_real, -g_imag], 1), jnp.concatenate([g_imag, g_real], 1)], 0
    )
    total = jnp.sum(jnp.sum(realified * realified, axis=1, keepdims=True), axis=0, keepdims=True)
    return realified / jnp.sqrt(total + 1e-06)


def product(a, b):
    return jnp.dot(a, b, precision=lax.Precision.HIGHEST, preferred_element_type=jnp.float32)


def project_kernel(packed_ref, inner_ref, near_ref, far_ref, out_ref, zt, out, in_sem, out_sem):
    n = zt.shape[1] // CHUNK
    halves = lambda ref: [ref.at[:, : ref.shape[1] // 2], ref.at[:, ref.shape[1] // 2 :]]
    (near_low, near_high), (far_low, far_high) = halves(near_ref), halves(far_ref)
    fetches, start = [], 0
    for k, piece in enumerate([far_low, near_low, inner_ref, near_high, far_high]):
        stop = start + piece.shape[1]
        fetches.append(pltpu.make_async_copy(piece, zt.at[:, start:stop], in_sem.at[k]))
        start = stop
    for fetch in fetches:
        fetch.start()

    def send(c):
        s = pl.ds(c * CHUNK, CHUNK)
        return pltpu.make_async_copy(out.at[:, s], out_ref.at[:, s], out_sem.at[c])

    size = 2 * BLK
    i = lax.broadcasted_iota(jnp.int32, (size, size), 0)
    j = lax.broadcasted_iota(jnp.int32, (size, size), 1)
    eye = jnp.where(i == j, 1.5, 0.0)
    packed = packed_ref[...]
    ys = [whiten_packed(packed[:, f * BLK : (f + 1) * BLK]) for f in range(FREQ)]
    cs = [eye - 0.5 * y for y in ys]
    ys = [product(y, c) for y, c in zip(ys, cs)]
    xs = cs
    for step in range(1, ITERS):
        cs = [eye - 0.5 * product(x, y) for x, y in zip(xs, ys)]
        if step < ITERS - 1:
            ys = [product(y, c) for y, c in zip(ys, cs)]
        xs = [product(c, x) for c, x in zip(cs, xs)]
    projectors = []
    for x in xs:
        top = x.T[:RANK]
        re, im = top[:, :BLK], top[:, BLK:]
        projectors.append(
            jnp.concatenate(
                [jnp.concatenate([re, -im], 1), jnp.concatenate([im, re], 1)], 0
            ).astype(jnp.bfloat16)
        )
    for fetch in fetches:
        fetch.wait()
    wide = 2 * RANK
    for c in range(n):
        s = slice(c * CHUNK, (c + 1) * CHUNK)
        for f in range(FREQ):
            out[f * wide : (f + 1) * wide, s] = jnp.dot(
                projectors[f], zt[f * size : (f + 1) * size, s], preferred_element_type=jnp.float32
            ).astype(jnp.bfloat16)
        send(c).start()
    for c in range(n):
        send(c).wait()


def all_sum(value, axis):
    n = lax.axis_size(axis)
    others = [lax.ppermute(value, axis, [(i, (i + k) % n) for i in range(n)]) for k in range(1, n)]
    for other in others:
        value = value + other
    return value


def local(spectra, mass_blocks, offsets, counts):
    rows, cols = spectra.shape[1:]
    blocks = rows // BS
    slots = mass_blocks.shape[2]
    devices = lax.axis_size(ROW)
    sp = spectra[0].reshape(blocks, BS, cols)
    up = [(i, i + 1) for i in range(devices - 1)]
    down = [(j, i) for i, j in up]
    far = HB - FAR
    near_before = lax.ppermute(sp[blocks - far :], ROW, up)
    near_after = lax.ppermute(sp[:far], ROW, down)
    far_before = lax.ppermute(sp[blocks - HB : blocks - far], ROW, up)
    far_after = lax.ppermute(sp[far:HB], ROW, down)

    rel = counts - lax.axis_index(ROW) * rows
    place = jnp.arange(blocks, dtype=jnp.int32)[None, :] + offsets[0].T
    index = jnp.where(place * BS < rel[0], place + HB, blocks + 2 * HB).astype(jnp.int32)
    mass = mass_blocks[0]
    inner = blocks - 2 * HB
    anywhere = pl.BlockSpec(memory_space=pl.ANY)
    scalars = pl.BlockSpec(memory_space=pltpu.SMEM)
    near = pl.BlockSpec(memory_space=pltpu.VMEM)
    gram_shape = (FREQ, 2 * BLK, 2 * BLK)
    xs_type = pltpu.VMEM((blocks + 2 * HB + 1, BS, cols), jnp.bfloat16)
    zt_inner = (cols, inner * BS)
    hold = lambda value: pltpu.with_memory_space_constraint(value, pltpu.VMEM)

    zt_in, part, xs, edge = pl.pallas_call(
        inner_kernel,
        out_shape=(
            pltpu.HBM(zt_inner, jnp.bfloat16),
            pltpu.VMEM(gram_shape, jnp.float32),
            xs_type,
            pltpu.VMEM((2 * HB, slots, BS, BS), jnp.bfloat16),
        ),
        in_specs=[scalars, scalars, anywhere, anywhere],
        out_specs=[anywhere] + [near] * 3,
        scratch_shapes=[
            pltpu.VMEM((inner, slots, BS, BS), jnp.bfloat16),
            pltpu.VMEM(zt_inner, jnp.bfloat16),
            pltpu.SemaphoreType.DMA,
            pltpu.SemaphoreType.DMA((inner // GROUP,)),
            pltpu.SemaphoreType.DMA((2,)),
            pltpu.SemaphoreType.DMA((inner // GROUP,)),
        ],
        compiler_params=pltpu.CompilerParams(vmem_limit_bytes=16 << 20),
        name="inner_rows",
    )(index, rel, pltpu.with_memory_space_constraint(mass, pltpu.HBM), pltpu.with_memory_space_constraint(sp, pltpu.HBM))

    def edges(lo, stride, groups, prev, nxt, start, result, held):
        shape = (cols, groups * GROUP * BS)
        return pl.pallas_call(
            functools.partial(edge_kernel, groups, lo, stride, prev.shape[0]),
            out_shape=(xs_type, pltpu.HBM(shape, jnp.bfloat16), result),
            in_specs=[scalars, scalars, near, anywhere, anywhere, near, near],
            out_specs=[near, anywhere, near],
            scratch_shapes=[
                pltpu.VMEM(gram_shape, jnp.float32),
                pltpu.VMEM(shape, jnp.bfloat16),
                pltpu.SemaphoreType.DMA((2,)),
                pltpu.SemaphoreType.DMA((groups,)),
            ],
            input_output_aliases={6: 0},
            compiler_params=pltpu.CompilerParams(vmem_limit_bytes=10 << 20),
            name="edge_rows",
        )(index, rel, hold(edge), prev, nxt, hold(start), hold(held))

    sides = HB // GROUP
    xs, zt_near, part = edges(
        1, 1, 2 * sides - 2, near_before, near_after, part, pltpu.VMEM(gram_shape, jnp.float32), xs
    )
    _, zt_far, packed = edges(
        0, 2 * sides - 1, 2, far_before, far_after, part, jax.ShapeDtypeStruct((BLK, 2 * BLK), jnp.float32), xs
    )

    for axis in ("c", "y", "x", "z"):
        packed = all_sum(packed, axis)

    count = rows // CHUNK
    out_rows = FREQ * 2 * RANK
    modes = pl.pallas_call(
        project_kernel,
        out_shape=jax.ShapeDtypeStruct((out_rows, rows), jnp.bfloat16),
        in_specs=[near, anywhere, anywhere, anywhere],
        out_specs=anywhere,
        scratch_shapes=[
            pltpu.VMEM((cols, rows), jnp.bfloat16),
            pltpu.VMEM((out_rows, rows), jnp.bfloat16),
            pltpu.SemaphoreType.DMA((5,)),
            pltpu.SemaphoreType.DMA((count,)),
        ],
        name="whiten_project",
    )(packed, zt_in, zt_near, zt_far)
    return modes.T[None]


def solution(mesh):
    finer = Mesh(mesh.devices.reshape(4, 2, 4, 4), ("z", "c", "x", "y"))
    return jax.shard_map(
        local,
        mesh=finer,
        in_specs=(
            P(SUB, ROW, None),
            P(SUB, ROW, None, None, None),
            P(SUB, ROW, None),
            P(SUB),
        ),
        out_specs=P(SUB, ROW, None),
        check_vma=False,
    )
```

```python
import functools

import jax
import jax.numpy as jnp
from jax import lax
from jax.experimental import pallas as pl
from jax.experimental.pallas import tpu as pltpu
from jax.sharding import Mesh
from jax.sharding import PartitionSpec as P

BLK = 64
RANK = 48
FREQ = 2
ITERS = 5
HB = 16
BS = 128
GROUP = 4
FAR = 4
CHUNK = 1024
SUB = ("z", "c")
ROW = ("x", "y")


def cut_block(rel, xs, spans):
    end = rel + HB * BS
    cut = lax.shift_right_arithmetic(end, 7)
    kept = jnp.bitwise_and(end, BS - 1)
    inside = functools.reduce(jnp.logical_or, [(cut >= lo) & (cut < hi) for lo, hi in spans])

    @pl.when((kept > 0) & inside)
    def _():
        rows = lax.broadcasted_iota(jnp.int32, xs.shape[1:], 0)
        block = xs[cut]
        xs[cut] = jnp.where(rows < kept, block, jnp.zeros_like(block))


def sender(zt, zt_ref, sem, g):
    return pltpu.make_async_copy(zt.at[g], zt_ref.at[g], sem.at[g])


def weigh_group(idx_ref, rel, first, g, mass, xs, zt_ref, gram):
    slots = mass.shape[1]
    rows = lax.broadcasted_iota(jnp.int32, (BS, xs.shape[2]), 0)
    parts = []
    for r in range(GROUP):
        b = first + r
        left = jnp.concatenate([mass[r, k] for k in range(slots)], axis=1)
        right = jnp.concatenate([xs[idx_ref[k, b]] for k in range(slots)], axis=0)
        acc = jnp.dot(left, right, preferred_element_type=jnp.float32)
        parts.append(jnp.where(rows < rel - b * BS, acc, 0.0).astype(jnp.bfloat16))
    z = jnp.concatenate(parts, axis=0)
    zt = z.T
    zt_ref[g] = zt
    for f in range(FREQ):
        s = slice(f * 2 * BLK, (f + 1) * 2 * BLK)
        gram[f] += jnp.dot(zt[s], z[:, s], preferred_element_type=jnp.float32)


def inner_kernel(idx_ref, rel_ref, mass_ref, sp_ref, zt_ref, gram_ref, xs, edge, mass, zt, x_sem, sem, edge_sem, out_sem):
    rel = rel_ref[0]
    local = sp_ref.shape[0]
    groups = mass.shape[0] // GROUP

    fetch_x = pltpu.make_async_copy(sp_ref, xs.at[pl.ds(HB, local)], x_sem)

    def fetch(g):
        return pltpu.make_async_copy(
            mass_ref.at[pl.ds(HB + g * GROUP, GROUP)], mass.at[pl.ds(g * GROUP, GROUP)], sem.at[g]
        )

    sides = [
        pltpu.make_async_copy(mass_ref.at[pl.ds(0, HB)], edge.at[pl.ds(0, HB)], edge_sem.at[0]),
        pltpu.make_async_copy(
            mass_ref.at[pl.ds(local - HB, HB)], edge.at[pl.ds(HB, HB)], edge_sem.at[1]
        ),
    ]
    fetch_x.start()
    for g in range(groups):
        fetch(g).start()
    for side in sides:
        side.start()
    gram_ref[...] = jnp.zeros_like(gram_ref)
    spare = xs.shape[0] - 1
    xs[spare] = jnp.zeros(xs.shape[1:], xs.dtype)
    fetch_x.wait()
    cut_block(rel, xs, [(HB, HB + local)])

    @pl.loop(0, groups)
    def _(g):
        fetch(g).wait()
        weigh_group(
            idx_ref, rel, HB + g * GROUP, g, mass.at[pl.ds(g * GROUP, GROUP)], xs, zt, gram_ref
        )
        sender(zt, zt_ref, out_sem, g).start()

    for side in sides:
        side.wait()
    for g in range(groups):
        sender(zt, zt_ref, out_sem, g).wait()


def edge_kernel(
    groups, lo, stride, width, idx_ref, rel_ref, edge, prev_ref, next_ref, part_ref, xs_in, xs, zt_ref, gram_ref, gram, zt, sem, out_sem
):
    del xs_in
    rel = rel_ref[0]
    local = xs.shape[0] - 1 - 2 * HB
    low = 0 if width == FAR else FAR
    high = HB + local + (HB - FAR if width == FAR else 0)
    copies = [
        pltpu.make_async_copy(prev_ref, xs.at[pl.ds(low, width)], sem.at[0]),
        pltpu.make_async_copy(next_ref, xs.at[pl.ds(high, width)], sem.at[1]),
    ]
    for copy in copies:
        copy.start()
    gram[...] = part_ref[...]
    for copy in copies:
        copy.wait()
    cut_block(rel, xs, [(low, low + width), (high, high + width)])

    @pl.loop(0, groups)
    def _(g):
        place = lo + g * stride
        first = jnp.where(place < HB // GROUP, place * GROUP, local - 2 * HB + place * GROUP)
        weigh_group(idx_ref, rel, first, g, edge.at[pl.ds(place * GROUP, GROUP)], xs, zt, gram)
        sender(zt, zt_ref, out_sem, g).start()

    if width == FAR:
        gram_ref[...] = pack(gram)
    else:
        gram_ref[...] = gram[...]
    for g in range(groups):
        sender(zt, zt_ref, out_sem, g).wait()


def pack(gram):
    i = lax.broadcasted_iota(jnp.int32, (BLK, BLK), 0)
    j = lax.broadcasted_iota(jnp.int32, (BLK, BLK), 1)
    packs = []
    for f in range(FREQ):
        h = gram[f]
        g_real = h[:BLK, :BLK] + h[BLK:, BLK:]
        g_imag = h[:BLK, BLK:] - h[BLK:, :BLK]
        packs.append(jnp.where(i <= j, g_real, g_imag))
    return jnp.concatenate(packs, axis=1)


def whiten_packed(packed):
    i = lax.broadcasted_iota(jnp.int32, (BLK, BLK), 0)
    j = lax.broadcasted_iota(jnp.int32, (BLK, BLK), 1)
    turned = packed.T
    g_real = jnp.where(i <= j, packed, turned)
    g_imag = jnp.where(i > j, packed, jnp.where(i < j, -turned, 0.0))
    realified = jnp.concatenate(
        [jnp.concatenate([g_real, -g_imag], 1), jnp.concatenate([g_imag, g_real], 1)], 0
    )
    total = jnp.sum(jnp.sum(realified * realified, axis=1, keepdims=True), axis=0, keepdims=True)
    return realified / jnp.sqrt(total + 1e-06)


def product(a, b):
    return jnp.dot(a, b, precision=lax.Precision.HIGHEST, preferred_element_type=jnp.float32)


def project_kernel(sums, inner_ref, near_ref, far_ref, out_ref, zt, out, in_sem, out_sem):
    n = out.shape[1] // CHUNK
    halves = lambda ref: [ref.at[: ref.shape[0] // 2], ref.at[ref.shape[0] // 2 :]]
    (near_low, near_high), (far_low, far_high) = halves(near_ref), halves(far_ref)
    fetches, start = [], 0
    for k, piece in enumerate([far_low, near_low, inner_ref, near_high, far_high]):
        stop = start + piece.shape[0]
        fetches.append(pltpu.make_async_copy(piece, zt.at[start:stop], in_sem.at[k]))
        start = stop
    for fetch in fetches:
        fetch.start()

    def send(c):
        s = pl.ds(c * CHUNK, CHUNK)
        return pltpu.make_async_copy(out.at[:, s], out_ref.at[:, s], out_sem.at[c])

    size = 2 * BLK
    i = lax.broadcasted_iota(jnp.int32, (size, size), 0)
    j = lax.broadcasted_iota(jnp.int32, (size, size), 1)
    eye = jnp.where(i == j, 1.5, 0.0)
    packed = sums[0][...]
    for other in sums[1:]:
        packed = packed + other[...]
    ys = [whiten_packed(packed[:, f * BLK : (f + 1) * BLK]) for f in range(FREQ)]
    cs = [eye - 0.5 * y for y in ys]
    ys = [product(y, c) for y, c in zip(ys, cs)]
    xs = cs
    for step in range(1, ITERS):
        cs = [eye - 0.5 * product(x, y) for x, y in zip(xs, ys)]
        if step < ITERS - 1:
            ys = [product(y, c) for y, c in zip(ys, cs)]
        xs = [product(c, x) for c, x in zip(cs, xs)]
    projectors = []
    for x in xs:
        top = x.T[:RANK]
        re, im = top[:, :BLK], top[:, BLK:]
        projectors.append(
            jnp.concatenate(
                [jnp.concatenate([re, -im], 1), jnp.concatenate([im, re], 1)], 0
            ).astype(jnp.bfloat16)
        )
    for fetch in fetches:
        fetch.wait()
    wide = 2 * RANK
    width = zt.shape[2]
    for c in range(n):
        for g in range(c * CHUNK // width, (c + 1) * CHUNK // width):
            for f in range(FREQ):
                out[f * wide : (f + 1) * wide, g * width : (g + 1) * width] = jnp.dot(
                    projectors[f],
                    zt[g, f * size : (f + 1) * size],
                    preferred_element_type=jnp.float32,
                ).astype(jnp.bfloat16)
        send(c).start()
    for c in range(n):
        send(c).wait()


def others(value, axis):
    n = lax.axis_size(axis)
    return [lax.ppermute(value, axis, [(i, (i + k) % n) for i in range(n)]) for k in range(1, n)]


def local(spectra, mass_blocks, offsets, counts):
    rows, cols = spectra.shape[1:]
    blocks = rows // BS
    slots = mass_blocks.shape[2]
    devices = lax.axis_size(ROW)
    sp = spectra[0].reshape(blocks, BS, cols)
    up = [(i, i + 1) for i in range(devices - 1)]
    down = [(j, i) for i, j in up]
    far = HB - FAR
    near_before = lax.ppermute(sp[blocks - far :], ROW, up)
    near_after = lax.ppermute(sp[:far], ROW, down)
    far_before = lax.ppermute(sp[blocks - HB : blocks - far], ROW, up)
    far_after = lax.ppermute(sp[far:HB], ROW, down)

    rel = counts - lax.axis_index(ROW) * rows
    place = jnp.arange(blocks, dtype=jnp.int32)[None, :] + offsets[0].T
    index = jnp.where(place * BS < rel[0], place + HB, blocks + 2 * HB).astype(jnp.int32)
    mass = mass_blocks[0]
    inner = blocks - 2 * HB
    anywhere = pl.BlockSpec(memory_space=pl.ANY)
    scalars = pl.BlockSpec(memory_space=pltpu.SMEM)
    near = pl.BlockSpec(memory_space=pltpu.VMEM)
    gram_shape = (FREQ, 2 * BLK, 2 * BLK)
    xs_type = pltpu.VMEM((blocks + 2 * HB + 1, BS, cols), jnp.bfloat16)
    zt_inner = (inner // GROUP, cols, GROUP * BS)
    hold = lambda value: pltpu.with_memory_space_constraint(value, pltpu.VMEM)

    zt_in, part, xs, edge = pl.pallas_call(
        inner_kernel,
        out_shape=(
            pltpu.HBM(zt_inner, jnp.bfloat16),
            pltpu.VMEM(gram_shape, jnp.float32),
            xs_type,
            pltpu.VMEM((2 * HB, slots, BS, BS), jnp.bfloat16),
        ),
        in_specs=[scalars, scalars, anywhere, anywhere],
        out_specs=[anywhere] + [near] * 3,
        scratch_shapes=[
            pltpu.VMEM((inner, slots, BS, BS), jnp.bfloat16),
            pltpu.VMEM(zt_inner, jnp.bfloat16),
            pltpu.SemaphoreType.DMA,
            pltpu.SemaphoreType.DMA((inner // GROUP,)),
            pltpu.SemaphoreType.DMA((2,)),
            pltpu.SemaphoreType.DMA((inner // GROUP,)),
        ],
        compiler_params=pltpu.CompilerParams(vmem_limit_bytes=16 << 20),
        name="inner_rows",
    )(index, rel, pltpu.with_memory_space_constraint(mass, pltpu.HBM), pltpu.with_memory_space_constraint(sp, pltpu.HBM))

    def edges(lo, stride, groups, prev, nxt, start, result, held):
        shape = (groups, cols, GROUP * BS)
        return pl.pallas_call(
            functools.partial(edge_kernel, groups, lo, stride, prev.shape[0]),
            out_shape=(xs_type, pltpu.HBM(shape, jnp.bfloat16), result),
            in_specs=[scalars, scalars, near, anywhere, anywhere, near, near],
            out_specs=[near, anywhere, near],
            scratch_shapes=[
                pltpu.VMEM(gram_shape, jnp.float32),
                pltpu.VMEM(shape, jnp.bfloat16),
                pltpu.SemaphoreType.DMA((2,)),
                pltpu.SemaphoreType.DMA((groups,)),
            ],
            input_output_aliases={6: 0},
            compiler_params=pltpu.CompilerParams(vmem_limit_bytes=10 << 20),
            name="edge_rows",
        )(index, rel, hold(edge), prev, nxt, hold(start), hold(held))

    sides = HB // GROUP
    xs, zt_near, part = edges(
        1, 1, 2 * sides - 2, near_before, near_after, part, pltpu.VMEM(gram_shape, jnp.float32), xs
    )
    _, zt_far, packed = edges(
        0, 2 * sides - 1, 2, far_before, far_after, part, jax.ShapeDtypeStruct((BLK, 2 * BLK), jnp.float32), xs
    )

    for axis in ("c", "y", "x"):
        packed = sum(others(packed, axis), packed)
    sums = [packed, *others(packed, "z")]

    count = rows // CHUNK
    out_rows = FREQ * 2 * RANK
    modes = pl.pallas_call(
        project_kernel,
        out_shape=jax.ShapeDtypeStruct((out_rows, rows), jnp.bfloat16),
        in_specs=[[near] * len(sums), anywhere, anywhere, anywhere],
        out_specs=anywhere,
        scratch_shapes=[
            pltpu.VMEM((blocks // GROUP, cols, GROUP * BS), jnp.bfloat16),
            pltpu.VMEM((out_rows, rows), jnp.bfloat16),
            pltpu.SemaphoreType.DMA((5,)),
            pltpu.SemaphoreType.DMA((count,)),
        ],
        name="whiten_project",
    )(sums, zt_in, zt_near, zt_far)
    return modes.T[None]


def solution(mesh):
    finer = Mesh(mesh.devices.reshape(4, 2, 4, 4), ("z", "c", "x", "y"))
    return jax.shard_map(
        local,
        mesh=finer,
        in_specs=(
            P(SUB, ROW, None),
            P(SUB, ROW, None, None, None),
            P(SUB, ROW, None),
            P(SUB),
        ),
        out_specs=P(SUB, ROW, None),
        check_vma=False,
    )
```

```python
import functools

import jax
import jax.numpy as jnp
from jax import lax
from jax.experimental import pallas as pl
from jax.experimental.pallas import tpu as pltpu
from jax.sharding import Mesh
from jax.sharding import PartitionSpec as P

BLK = 64
RANK = 48
FREQ = 2
ITERS = 5
HB = 16
BS = 128
GROUP = 4
FAR = 4
CHUNK = 1024
SUB = ("z", "c")
ROW = ("x", "y")


def cut_block(rel, xs, spans):
    end = rel + HB * BS
    cut = lax.shift_right_arithmetic(end, 7)
    kept = jnp.bitwise_and(end, BS - 1)
    inside = functools.reduce(jnp.logical_or, [(cut >= lo) & (cut < hi) for lo, hi in spans])

    @pl.when((kept > 0) & inside)
    def _():
        rows = lax.broadcasted_iota(jnp.int32, xs.shape[1:], 0)
        block = xs[cut]
        xs[cut] = jnp.where(rows < kept, block, jnp.zeros_like(block))


def sender(zt, zt_ref, sem, g):
    return pltpu.make_async_copy(zt.at[g], zt_ref.at[g], sem.at[g])


def weigh_group(idx_ref, rel, first, g, mass, xs, zt_ref, gram):
    slots = mass.shape[1]
    rows = lax.broadcasted_iota(jnp.int32, (BS, xs.shape[2]), 0)
    parts = []
    for r in range(GROUP):
        b = first + r
        left = jnp.concatenate([mass[r, k] for k in range(slots)], axis=1)
        right = jnp.concatenate([xs[idx_ref[k, b]] for k in range(slots)], axis=0)
        acc = jnp.dot(left, right, preferred_element_type=jnp.float32)
        parts.append(jnp.where(rows < rel - b * BS, acc, 0.0).astype(jnp.bfloat16))
    z = jnp.concatenate(parts, axis=0)
    zt = z.T
    zt_ref[g] = zt
    for f in range(FREQ):
        s = slice(f * 2 * BLK, (f + 1) * 2 * BLK)
        gram[f] += jnp.dot(zt[s], z[:, s], preferred_element_type=jnp.float32)


def inner_kernel(idx_ref, rel_ref, mass_ref, sp_ref, zt_ref, gram_ref, xs, edge, mass, zt, x_sem, sem, edge_sem, out_sem):
    rel = rel_ref[0]
    local = sp_ref.shape[0]
    groups = mass.shape[0] // GROUP

    fetch_x = pltpu.make_async_copy(sp_ref, xs.at[pl.ds(HB, local)], x_sem)

    def fetch(g):
        return pltpu.make_async_copy(
            mass_ref.at[pl.ds(HB + g * GROUP, GROUP)], mass.at[pl.ds(g * GROUP, GROUP)], sem.at[g]
        )

    sides = [
        pltpu.make_async_copy(mass_ref.at[pl.ds(0, HB)], edge.at[pl.ds(0, HB)], edge_sem.at[0]),
        pltpu.make_async_copy(
            mass_ref.at[pl.ds(local - HB, HB)], edge.at[pl.ds(HB, HB)], edge_sem.at[1]
        ),
    ]
    fetch_x.start()
    for g in range(groups):
        fetch(g).start()
    for side in sides:
        side.start()
    gram_ref[...] = jnp.zeros_like(gram_ref)
    spare = xs.shape[0] - 1
    xs[spare] = jnp.zeros(xs.shape[1:], xs.dtype)
    fetch_x.wait()
    cut_block(rel, xs, [(HB, HB + local)])

    @pl.loop(0, groups)
    def _(g):
        fetch(g).wait()
        weigh_group(
            idx_ref, rel, HB + g * GROUP, g, mass.at[pl.ds(g * GROUP, GROUP)], xs, zt, gram_ref
        )
        sender(zt, zt_ref, out_sem, g).start()

    for side in sides:
        side.wait()
    for g in range(groups):
        sender(zt, zt_ref, out_sem, g).wait()


def edge_kernel(
    groups, lo, stride, width, idx_ref, rel_ref, edge, prev_ref, next_ref, part_ref, xs_in, xs, zt_ref, gram_ref, gram, zt, sem, out_sem
):
    del xs_in
    rel = rel_ref[0]
    local = xs.shape[0] - 1 - 2 * HB
    low = 0 if width == FAR else FAR
    high = HB + local + (HB - FAR if width == FAR else 0)
    copies = [
        pltpu.make_async_copy(prev_ref, xs.at[pl.ds(low, width)], sem.at[0]),
        pltpu.make_async_copy(next_ref, xs.at[pl.ds(high, width)], sem.at[1]),
    ]
    for copy in copies:
        copy.start()
    gram[...] = part_ref[...]
    for copy in copies:
        copy.wait()
    cut_block(rel, xs, [(low, low + width), (high, high + width)])

    @pl.loop(0, groups)
    def _(g):
        place = lo + g * stride
        first = jnp.where(place < HB // GROUP, place * GROUP, local - 2 * HB + place * GROUP)
        weigh_group(idx_ref, rel, first, g, edge.at[pl.ds(place * GROUP, GROUP)], xs, zt, gram)
        sender(zt, zt_ref, out_sem, g).start()

    if width == FAR:
        gram_ref[...] = pack(gram)
    else:
        gram_ref[...] = gram[...]
    for g in range(groups):
        sender(zt, zt_ref, out_sem, g).wait()


def pack(gram):
    i = lax.broadcasted_iota(jnp.int32, (BLK, BLK), 0)
    j = lax.broadcasted_iota(jnp.int32, (BLK, BLK), 1)
    packs = []
    for f in range(FREQ):
        h = gram[f]
        g_real = h[:BLK, :BLK] + h[BLK:, BLK:]
        g_imag = h[:BLK, BLK:] - h[BLK:, :BLK]
        packs.append(jnp.where(i <= j, g_real, g_imag))
    return jnp.concatenate(packs, axis=1)


def whiten_packed(packed):
    i = lax.broadcasted_iota(jnp.int32, (BLK, BLK), 0)
    j = lax.broadcasted_iota(jnp.int32, (BLK, BLK), 1)
    turned = packed.T
    g_real = jnp.where(i <= j, packed, turned)
    g_imag = jnp.where(i > j, packed, jnp.where(i < j, -turned, 0.0))
    realified = jnp.concatenate(
        [jnp.concatenate([g_real, -g_imag], 1), jnp.concatenate([g_imag, g_real], 1)], 0
    )
    total = jnp.sum(jnp.sum(realified * realified, axis=1, keepdims=True), axis=0, keepdims=True)
    return realified / jnp.sqrt(total + 1e-06)


def product(a, b):
    return jnp.dot(a, b, precision=lax.Precision.HIGHEST, preferred_element_type=jnp.float32)


def project_kernel(sums, inner_ref, near_ref, far_ref, out_ref, zt, out, in_sem, out_sem):
    n = out.shape[1] // CHUNK
    halves = lambda ref: [ref.at[: ref.shape[0] // 2], ref.at[ref.shape[0] // 2 :]]
    (near_low, near_high), (far_low, far_high) = halves(near_ref), halves(far_ref)
    fetches, start = [], 0
    for k, piece in enumerate([far_low, near_low, inner_ref, near_high, far_high]):
        stop = start + piece.shape[0]
        fetches.append(pltpu.make_async_copy(piece, zt.at[start:stop], in_sem.at[k]))
        start = stop
    for fetch in fetches:
        fetch.start()

    def send(c):
        s = pl.ds(c * CHUNK, CHUNK)
        return pltpu.make_async_copy(out.at[:, s], out_ref.at[:, s], out_sem.at[c])

    size = 2 * BLK
    i = lax.broadcasted_iota(jnp.int32, (size, size), 0)
    j = lax.broadcasted_iota(jnp.int32, (size, size), 1)
    eye = jnp.where(i == j, 1.5, 0.0)
    packed = sums[0][...]
    for other in sums[1:]:
        packed = packed + other[...]
    ys = [whiten_packed(packed[:, f * BLK : (f + 1) * BLK]) for f in range(FREQ)]
    cs = [eye - 0.5 * y for y in ys]
    ys = [product(y, c) for y, c in zip(ys, cs)]
    xs = cs
    for step in range(1, ITERS):
        cs = [eye - 0.5 * product(x, y) for x, y in zip(xs, ys)]
        if step < ITERS - 1:
            ys = [product(y, c) for y, c in zip(ys, cs)]
        xs = [product(c, x) for c, x in zip(cs, xs)]
    projectors = []
    for x in xs:
        top = x.T[:RANK]
        re, im = top[:, :BLK], top[:, BLK:]
        projectors.append(
            jnp.concatenate(
                [jnp.concatenate([re, -im], 1), jnp.concatenate([im, re], 1)], 0
            ).astype(jnp.bfloat16)
        )
    for fetch in fetches:
        fetch.wait()
    wide = 2 * RANK
    width = zt.shape[2]
    for c in range(n):
        for g in range(c * CHUNK // width, (c + 1) * CHUNK // width):
            for f in range(FREQ):
                out[f * wide : (f + 1) * wide, g * width : (g + 1) * width] = jnp.dot(
                    projectors[f],
                    zt[g, f * size : (f + 1) * size],
                    preferred_element_type=jnp.float32,
                ).astype(jnp.bfloat16)
        send(c).start()
    for c in range(n):
        send(c).wait()


def others(value, axis):
    n = lax.axis_size(axis)
    return [lax.ppermute(value, axis, [(i, (i + k) % n) for i in range(n)]) for k in range(1, n)]


def local(spectra, mass_blocks, offsets, counts):
    rows, cols = spectra.shape[1:]
    blocks = rows // BS
    slots = mass_blocks.shape[2]
    devices = lax.axis_size(ROW)
    sp = spectra[0].reshape(blocks, BS, cols)
    up = [(i, i + 1) for i in range(devices - 1)]
    down = [(j, i) for i, j in up]
    far = HB - FAR
    near_before = lax.ppermute(sp[blocks - far :], ROW, up)
    near_after = lax.ppermute(sp[:far], ROW, down)
    far_before = lax.ppermute(sp[blocks - HB : blocks - far], ROW, up)
    far_after = lax.ppermute(sp[far:HB], ROW, down)

    rel = counts - lax.axis_index(ROW) * rows
    place = jnp.arange(blocks, dtype=jnp.int32)[None, :] + offsets[0].T
    index = jnp.where(place * BS < rel[0], place + HB, blocks + 2 * HB).astype(jnp.int32)
    mass = mass_blocks[0]
    inner = blocks - 2 * HB
    anywhere = pl.BlockSpec(memory_space=pl.ANY)
    scalars = pl.BlockSpec(memory_space=pltpu.SMEM)
    near = pl.BlockSpec(memory_space=pltpu.VMEM)
    gram_shape = (FREQ, 2 * BLK, 2 * BLK)
    xs_type = pltpu.VMEM((blocks + 2 * HB + 1, BS, cols), jnp.bfloat16)
    zt_inner = (inner // GROUP, cols, GROUP * BS)
    hold = lambda value: pltpu.with_memory_space_constraint(value, pltpu.VMEM)

    zt_in, part, xs, edge = pl.pallas_call(
        inner_kernel,
        out_shape=(
            pltpu.HBM(zt_inner, jnp.bfloat16),
            pltpu.VMEM(gram_shape, jnp.float32),
            xs_type,
            pltpu.VMEM((2 * HB, slots, BS, BS), jnp.bfloat16),
        ),
        in_specs=[scalars, scalars, anywhere, anywhere],
        out_specs=[anywhere] + [near] * 3,
        scratch_shapes=[
            pltpu.VMEM((inner, slots, BS, BS), jnp.bfloat16),
            pltpu.VMEM(zt_inner, jnp.bfloat16),
            pltpu.SemaphoreType.DMA,
            pltpu.SemaphoreType.DMA((inner // GROUP,)),
            pltpu.SemaphoreType.DMA((2,)),
            pltpu.SemaphoreType.DMA((inner // GROUP,)),
        ],
        compiler_params=pltpu.CompilerParams(vmem_limit_bytes=16 << 20),
        name="inner_rows",
    )(index, rel, pltpu.with_memory_space_constraint(mass, pltpu.HBM), pltpu.with_memory_space_constraint(sp, pltpu.HBM))

    def edges(lo, stride, groups, prev, nxt, start, result, held):
        shape = (groups, cols, GROUP * BS)
        return pl.pallas_call(
            functools.partial(edge_kernel, groups, lo, stride, prev.shape[0]),
            out_shape=(xs_type, pltpu.HBM(shape, jnp.bfloat16), result),
            in_specs=[scalars, scalars, near, anywhere, anywhere, near, near],
            out_specs=[near, anywhere, near],
            scratch_shapes=[
                pltpu.VMEM(gram_shape, jnp.float32),
                pltpu.VMEM(shape, jnp.bfloat16),
                pltpu.SemaphoreType.DMA((2,)),
                pltpu.SemaphoreType.DMA((groups,)),
            ],
            input_output_aliases={6: 0},
            compiler_params=pltpu.CompilerParams(vmem_limit_bytes=10 << 20),
            name="edge_rows",
        )(index, rel, hold(edge), prev, nxt, hold(start), hold(held))

    sides = HB // GROUP
    xs, zt_near, part = edges(
        1, 1, 2 * sides - 2, near_before, near_after, part, pltpu.VMEM(gram_shape, jnp.float32), xs
    )
    _, zt_far, packed = edges(
        0, 2 * sides - 1, 2, far_before, far_after, part, jax.ShapeDtypeStruct((BLK, 2 * BLK), jnp.float32), xs
    )

    for axis in ("c", "y", "x"):
        packed = sum(others(packed, axis), packed)
    sums = [packed, *others(packed, "z")]

    count = rows // CHUNK
    out_rows = FREQ * 2 * RANK
    modes = pl.pallas_call(
        project_kernel,
        out_shape=jax.ShapeDtypeStruct((out_rows, rows), jnp.bfloat16),
        in_specs=[[near] * len(sums), anywhere, anywhere, anywhere],
        out_specs=anywhere,
        scratch_shapes=[
            pltpu.VMEM((blocks // GROUP, cols, GROUP * BS), jnp.bfloat16),
            pltpu.VMEM((out_rows, rows), jnp.bfloat16),
            pltpu.SemaphoreType.DMA((5,)),
            pltpu.SemaphoreType.DMA((count,)),
        ],
        compiler_params=pltpu.CompilerParams(vmem_limit_bytes=12 << 20),
        name="whiten_project",
    )([hold(v) for v in sums], *(pltpu.with_memory_space_constraint(v, pltpu.HBM) for v in (zt_in, zt_near, zt_far)))
    return modes.T[None]


def solution(mesh):
    finer = Mesh(mesh.devices.reshape(4, 2, 4, 4), ("z", "c", "x", "y"))
    return jax.shard_map(
        local,
        mesh=finer,
        in_specs=(
            P(SUB, ROW, None),
            P(SUB, ROW, None, None, None),
            P(SUB, ROW, None),
            P(SUB),
        ),
        out_specs=P(SUB, ROW, None),
        check_vma=False,
    )
```
